256 devices in a mesh: dp: 4 (over x), expert: 64 (over z, y, core).
Axes of the slice: x: 4, y: 4, z: 8, core: 2. Of those that a mesh axis runs over, the one named last changes fastest.
Arguments:
- tokens: bfloat16 [32768, 3584], P(('dp', 'expert')), may hold values from -6 to 6
- out_grad: bfloat16 [32768, 3584], P(('dp', 'expert')), may hold values from -1.5 to 1.5
- route: int32 [32768, 8], P(('dp', 'expert')), may hold values from 0 to 255, all different within a row; in each aligned block of 128 rows (0 to 127, 128 to 255, ...) at most 8 rows name the same one
- gate_fixed: int32 [32768, 8], P(('dp', 'expert')), may hold values from 16 to 256
- w_gate: bfloat16 [64, 3584, 256], P('expert'), may hold values from -0.09375 to 0.09375
- w_up: bfloat16 [64, 3584, 256], P('expert'), may hold values from -0.09375 to 0.09375
- w_down: bfloat16 [64, 256, 3584], P('expert'), may hold values from -0.125 to 0.125
- router_bias: float32 [256], replicated, may hold values from -1 to 1
- loads: int32 [256, 256], P(('dp', 'expert')), may hold values from 0 to 189
Outputs:
- token_grad: bfloat16 [32768, 3584], P(('dp', 'expert'))
- gate_grad: float32 [32768, 8], P(('dp', 'expert'))
- grad_gate: bfloat16 [64, 3584, 256], P('expert', 'dp')
- grad_up: bfloat16 [64, 3584, 256], P('expert', 'dp')
- grad_down: bfloat16 [64, 256, 3584], P('expert', None, 'dp')
- new_bias: float32 [256], replicated
The draws below stay inside these ranges and needn't reach their ends.
Inputs may be any that keep to these rules, and one draw needn't show every extreme that they name: `route`: each row names 8 different experts. In the rows of one device no expert is named more than 8 times, a bound that some block reaches.
All inputs are finite; a program needn't handle non-finite values.
Results may differ from the reference program's by a relative error of at most 0.02.
Values may be sent and summed in bfloat16 or wider, within the bound.
A program may use at most 128 MiB of HBM per device.

```python
import math
import jax
import jax.numpy as jnp
import numpy as np
from jax import lax

D = 3584
FF = 2048
EXPERTS_ALL = 256
TOPK = 8
SPLIT = 8
TOK_DEV = 128
CAP = 8
F_DEV = 256
SOURCES = 256
TOKENS = 32768
N_EXPERT = 64


def draw_loads(key, part):
    base_counts = jax.random.randint(key, (SOURCES, EXPERTS_ALL), 0, 64, dtype=jnp.int32)
    base_counts = base_counts.at[SOURCES - 1, 0].set(63).at[0, 1].set(0)
    rising = (SOURCES - 1 + 2 * jnp.arange(SOURCES, dtype=jnp.int32))[:, None]
    return base_counts * rising // (SOURCES - 1)


def plant(values, key, smallest, high):
    dims = values.shape
    index_at = [jax.random.randint(jax.random.fold_in(key, axis), (), 0, dims[axis]) for axis in range(len(dims))]
    values = values.at[tuple(index_at)].set(smallest)
    longest = dims.index(max(dims))
    index_at[longest] = (index_at[longest] + 1) % dims[longest]
    return values.at[tuple(index_at)].set(high)


def block_levels(stream_key, dims, shards, least, top_value):
    factor_of = 1.0
    for position, blocks in shards:
        draws = jax.random.uniform(jax.random.fold_in(jax.random.fold_in(stream_key, 6), position), (blocks,), jnp.float32, least / len(shards), top_value / len(shards))
        factor_of = factor_of * jnp.repeat(jnp.exp(draws), dims[position] // blocks).reshape((-1,) + (1,) * (len(dims) - 1 - position))
    return factor_of


def shared_out(key, own, number, rows, number_of, top, limit, slope):
    ranking = jax.random.permutation(key, number_of)
    heavy_load, usual = load_shares(number_of, rows * top, limit, slope, True), load_shares(number_of, rows * top, limit, slope, False)
    places = jnp.arange(number_of)

    def named(tallies, offset_by):
        used = int((tallies > 0).sum())
        fixed = max(1, used // 4)
        shifted = fixed + (places - fixed + offset_by * (used - fixed)) % max(1, number_of - fixed)
        return jnp.zeros((number_of,), jnp.int32).at[ranking[jnp.where(places < fixed, places, shifted)]].set(jnp.asarray(tallies, jnp.int32))

    tallies = jnp.where(number % 4 == 0, named(heavy_load, number // 4), named(usual, number - number // 4 - 1))
    mixed = jax.random.permutation(jax.random.fold_in(own, 3), number_of)
    source_of, receiver = mixed[0:number_of // 2 * 2:2], mixed[1:number_of // 2 * 2:2]
    slack = jnp.minimum(tallies[source_of] - 1, limit - tallies[receiver]) // 2
    slack = jnp.where((source_of == ranking[0]) | (receiver == ranking[0]) | (tallies[receiver] == 0), 0, jnp.maximum(slack, 0))
    shifted = jax.random.randint(jax.random.fold_in(own, 4), (number_of // 2,), 0, 1 << 20) % (slack + 1)
    tallies = tallies.at[source_of].add(-shifted).at[receiver].add(shifted)
    items = jnp.searchsorted(jnp.cumsum(tallies), jnp.arange(rows * top), side="right").astype(jnp.int32)
    listing = items.reshape(top, rows).T
    listing = listing[jax.random.permutation(jax.random.fold_in(own, 1), rows)]
    offset_by = jax.random.randint(jax.random.fold_in(own, 2), (rows, 1), 0, top)
    return jnp.take_along_axis(listing, (jnp.arange(top)[None, :] + offset_by) % top, axis=1)


def load_shares(count, total, limit, skew, full):
    weights = [(1 << 20) // math.isqrt(rank ** skew) + 1 for rank in range(1, count + 1)]
    largest = limit if full else min(limit, max(-(-total // count), total * weights[0] // sum(weights)))
    least = 1 if total - largest >= count - 1 else 0
    counts, rest = [largest] + [least] * (count - 1), total - largest - least * (count - 1)
    while rest > 0:
        candidates = [i for i in range(1, count) if counts[i] < largest] or [i for i in range(1, count) if counts[i] < limit]
        whole, remaining = sum([weights[i] for i in candidates]), rest
        for i in candidates:
            extra = min(limit - counts[i], max(1, remaining * weights[i] // whole), rest)
            counts[i] = counts[i] + extra
            rest = rest - extra
    return np.array(counts)


def bell_draw(key, extent, deviation, most, cuts=(), held_as=jnp.bfloat16):
    values = deviation * jax.random.normal(key, extent, jnp.float32)
    if cuts:
        values = values * block_levels(key, extent, cuts, -0.22, 0.18)
    return jnp.clip(values, -most, most).astype(held_as)


def setup_inputs(seed: int = 0) -> dict:
    splits = jax.random.split(jax.random.key(seed), 10)
    tokens = bell_draw(splits[0], (TOKENS, D), 1.0, 6.0, ((0, 256),))
    out_grad = bell_draw(splits[1], (TOKENS, D), 0.25, 1.5, ((0, 256),))
    route_keys = jax.random.split(jax.random.fold_in(splits[2], 1), TOKENS // TOK_DEV)
    route_turns = jax.random.permutation(jax.random.fold_in(splits[2], 3), TOKENS // TOK_DEV)
    route = jax.vmap(lambda own, number: shared_out(jax.random.fold_in(splits[2], 2), own, number, TOK_DEV, EXPERTS_ALL, TOPK, CAP, 1))(route_keys, route_turns).reshape((TOKENS, TOPK))
    gate_fixed = plant(jax.random.randint(splits[3], (TOKENS, TOPK), 16, 257), jax.random.fold_in(splits[3], 1), 16, 256).astype(jnp.int32)
    w_gate = bell_draw(splits[4], (N_EXPERT, D, F_DEV), D ** -0.5, 0.09375, ((0, 64),))
    w_up = bell_draw(splits[5], (N_EXPERT, D, F_DEV), D ** -0.5, 0.09375, ((0, 64),))
    w_down = bell_draw(splits[6], (N_EXPERT, F_DEV, D), FF ** -0.5, 0.125, ((0, 64),))
    router_bias = jnp.clip(jax.random.uniform(splits[7], (EXPERTS_ALL,), jnp.float32, -1.0, 1.0), -1.0, 1.0)
    loads = draw_loads(jax.random.fold_in(splits[9], 71), 0)
    return dict(tokens=tokens, out_grad=out_grad, route=route, gate_fixed=gate_fixed, w_gate=w_gate, w_up=w_up, w_down=w_down, router_bias=router_bias, loads=loads)


bias_step = 0.125


def reference(tokens, out_grad, route, gate_fixed, w_gate, w_up, w_down, router_bias, loads):
    flights = N_EXPERT // SPLIT
    total = TOKENS * TOPK
    most_rows = SOURCES * CAP
    width = tokens.shape[1]
    flat_route = route.reshape(-1)
    flat_gate = gate_fixed.reshape(-1).astype(jnp.float32) / 256.0

    def one_expert(expert_id):
        picked = jnp.nonzero(flat_route == expert_id, size=most_rows, fill_value=total)[0].astype(jnp.int32)
        is_valid = picked < total
        safe_index = jnp.minimum(picked, total - 1)
        token_id = safe_index // TOPK
        rows_in = jnp.where(is_valid[:, None], tokens[token_id], jnp.zeros((), tokens.dtype))
        rows_grad = jnp.where(is_valid[:, None], out_grad[token_id], jnp.zeros((), out_grad.dtype))
        row_gate = jnp.where(is_valid, flat_gate[safe_index], jnp.zeros((), flat_gate.dtype))[:, None]
        first = (expert_id * SPLIT).astype(jnp.int32)
        gate_block = lax.dynamic_slice_in_dim(w_gate, first, SPLIT, 0)
        up_block = lax.dynamic_slice_in_dim(w_up, first, SPLIT, 0)
        down_block = lax.dynamic_slice_in_dim(w_down, first, SPLIT, 0)
        dx_sum = jnp.zeros((most_rows, width), jnp.float32)
        gate_sum = jnp.zeros((most_rows,), jnp.float32)
        grads_g = []
        grads_u = []
        grads_d = []
        for slice_id in range(SPLIT):
            gate_slice = gate_block[slice_id]
            up_slice = up_block[slice_id]
            down_slice = down_block[slice_id]
            pre_gate = jnp.dot(rows_in, gate_slice, preferred_element_type=jnp.float32)
            pre_up = jnp.dot(rows_in, up_slice, preferred_element_type=jnp.float32)
            sigmoid_gate = jax.nn.sigmoid(pre_gate)
            activated = pre_gate * sigmoid_gate
            hidden = activated * pre_up
            back_proj = jnp.dot(rows_grad, down_slice.T, preferred_element_type=jnp.float32)
            part_gate = jnp.sum(back_proj * hidden, axis=1).astype(jnp.bfloat16)
            grad_hidden = row_gate * back_proj
            grad_pregate = (grad_hidden * pre_up * sigmoid_gate * (1.0 + pre_gate * (1.0 - sigmoid_gate))).astype(jnp.bfloat16)
            grad_preup = (grad_hidden * activated).astype(jnp.bfloat16)
            scaled_hidden = (row_gate * hidden).astype(jnp.bfloat16)
            part_dx = (jnp.dot(grad_pregate, gate_slice.T, preferred_element_type=jnp.float32)
                       + jnp.dot(grad_preup, up_slice.T, preferred_element_type=jnp.float32)).astype(jnp.bfloat16)
            dx_sum = dx_sum + part_dx.astype(jnp.float32)
            gate_sum = gate_sum + part_gate.astype(jnp.float32)
            grads_g.append(jnp.dot(rows_in.T, grad_pregate, preferred_element_type=jnp.float32))
            grads_u.append(jnp.dot(rows_in.T, grad_preup, preferred_element_type=jnp.float32))
            grads_d.append(jnp.dot(scaled_hidden.T, rows_grad, preferred_element_type=jnp.float32))
        return dx_sum, gate_sum, picked, jnp.stack(grads_g), jnp.stack(grads_u), jnp.stack(grads_d)

    dx_rows, gate_rows, picked, grad_g, grad_u, grad_d = lax.map(one_expert, jnp.arange(flights, dtype=jnp.int32))
    picked = picked.reshape(-1)
    token_id = jnp.where(picked < total, picked // TOPK, TOKENS).astype(jnp.int32)
    token_grad = jax.ops.segment_sum(dx_rows.reshape(-1, width), token_id, num_segments=TOKENS).astype(jnp.bfloat16)
    gate_grad = jax.ops.segment_sum(gate_rows.reshape(-1), picked, num_segments=total).reshape(TOKENS, TOPK)
    grad_gate = grad_g.reshape(N_EXPERT, width, -1).astype(jnp.bfloat16)
    grad_up = grad_u.reshape(N_EXPERT, width, -1).astype(jnp.bfloat16)
    grad_down = grad_d.reshape(N_EXPERT, -1, width).astype(jnp.bfloat16)
    load = jnp.sum(loads, axis=0)
    overall = jnp.sum(load)
    new_bias = router_bias + bias_step * jnp.sign(overall - EXPERTS_ALL * load).astype(jnp.float32)
    return token_grad, gate_grad, grad_gate, grad_up, grad_down, new_bias
```

```python
import jax
import jax.numpy as jnp
from jax import lax
from jax.experimental import pallas as pl
from jax.experimental.pallas import tpu as pltpu
from jax.sharding import PartitionSpec as P

EXPERTS_ALL = 256
BIAS_STEP = 0.125
TOPK = 8
CAP = 8
NX = 4
NY = 4
NC = 2
NZ = 8
LANE = 128

Z_ORDER = (0, 1, 7, 2, 6, 3, 5, 4)
STEP_ROWS = NC * NY * CAP
GROUP_STEPS = 2
GROUPS = NZ // GROUP_STEPS
GROUP_ROWS = GROUP_STEPS * STEP_ROWS
ROWS = NZ * STEP_ROWS

MESH = pl.DeviceIdType.MESH
F32 = jnp.float32
BF16 = jnp.bfloat16


def dot(a, b):
    return lax.dot_general(a, b, (((1,), (0,)), ((), ())), preferred_element_type=F32)


def dot_nt(a, b):
    return lax.dot_general(a, b, (((1,), (1,)), ((), ())), preferred_element_type=F32)


def pick_rows(tokens_ref, grad_ref, route, gate, st, sg, sel_ref, hot_ref):
    count, width = tokens_ref.shape
    masks, gates = [], []
    for j in range(NZ):
        hit = (route == float(j)).astype(F32)
        hot_ref[j * TOPK : (j + 1) * TOPK, :] = hit
        masks.append(jnp.sum(hit, axis=0, keepdims=True))
        gates.append(jnp.sum(hit * gate, axis=0, keepdims=True))
    mask = jnp.concatenate(masks, axis=0)
    before = lax.broadcasted_iota(jnp.int32, (count, count), 0) < lax.broadcasted_iota(
        jnp.int32, (count, count), 1
    )
    place = dot(mask.astype(BF16), before.astype(F32).astype(BF16))
    slot = lax.broadcasted_iota(jnp.int32, (CAP, count), 0).astype(F32)
    picks, columns = [], []
    for j in range(NZ):
        pick = jnp.where(place[j : j + 1, :] == slot, 1.0, 0.0) * masks[j]
        picks.append(pick)
        columns.append(jnp.sum(pick * gates[j], axis=1, keepdims=True))
    sel = jnp.concatenate(picks, axis=0)
    column = jnp.concatenate(columns, axis=0)
    sel_ref[...] = sel
    one_hot = sel.astype(BF16)
    st[...] = dot(one_hot, tokens_ref[...]).astype(BF16).reshape(NZ, CAP, width)
    sg[:, :, :width] = dot(one_hot, grad_ref[...]).astype(BF16).reshape(NZ, CAP, width)
    wide = jnp.broadcast_to(column, (NZ * CAP, LANE)).astype(BF16)
    sg[:, :, width:] = wide.reshape(NZ, CAP, LANE)


def layer_kernel(
    tokens_ref,
    grad_ref,
    route_ref,
    gate_ref,
    loads_ref,
    wg_hbm,
    wu_hbm,
    wd_hbm,
    back_out,
    sel_ref,
    hot_ref,
    both_out,
    down_out,
    load_out,
    st,
    sg,
    xt,
    xg,
    tx,
    wg,
    wu,
    wd,
    gcat,
    gt,
    gx,
    dx_keep,
    dx_send,
    dx_got,
    py,
    rh,
    ry,
    zs,
    back,
    pb,
    pb_own,
    half,
    fin,
    lsum,
    lgot,
    zsend,
    zrecv,
    ysend,
    yrecv,
    csend,
    crecv,
    tsend,
    trecv,
    usend,
    urecv,
    gsend,
    grecv,
    dsend,
    drecv,
    rsend,
    rrecv,
    bsend,
    brecv,
    xsend,
    xrecv,
    lsend,
    lrecv,
    local,
):
    width = xt.shape[3]
    units = wg.shape[1]
    share = width // NX
    x = lax.axis_index("dp")
    e = lax.axis_index("expert")
    z = e // (NY * NC)
    y = (e // NC) % NY
    c = e % NC

    def at(dx=0, dz=0, dy=0, dc=0):
        there_z = (z + dz) % NZ
        there_y = (y + dy) % NY
        there_c = (c + dc) % NC
        return ((x + dx) % NX, there_z * (NY * NC) + there_y * NC + there_c)

    sent = []

    def send(src, dst, sems, n, **where):
        copy = pltpu.make_async_remote_copy(
            src_ref=src,
            dst_ref=dst,
            send_sem=sems[0].at[n],
            recv_sem=sems[1].at[n],
            device_id=at(**where),
            device_id_type=MESH,
        )
        copy.start()
        sent.append(copy)
        return copy

    def arrived(copies):
        for copy in copies:
            copy.wait_recv()

    weights = [
        pltpu.make_async_copy(a.at[0], b, local.at[n])
        for n, (a, b) in enumerate(((wg_hbm, wg), (wu_hbm, wu), (wd_hbm, wd)))
    ]
    for copy in weights:
        copy.start()

    peers = [dict(dc=1)]
    peers += [dict(dy=d) for d in range(1, NY)]
    peers += [dict(dz=d) for d in range(1, NZ)]
    peers += [dict(dx=d) for d in range(1, NX)]
    barrier = pltpu.get_barrier_semaphore()
    for peer in peers:
        pl.semaphore_signal(barrier, inc=1, device_id=at(**peer), device_id_type=MESH)

    lsum[0] = jnp.broadcast_to(loads_ref[...].astype(F32), lsum.shape[1:])
    pick_rows(
        tokens_ref,
        grad_ref,
        route_ref[...].astype(F32),
        gate_ref[...].astype(F32) * (1.0 / 256.0),
        st,
        sg,
        sel_ref,
        hot_ref,
    )
    pl.semaphore_wait(barrier, len(peers))

    kinds = ((st, xt), (sg, xg))

    def slot(r):
        return pl.ds(r * CAP, CAP)

    own = []
    for kind, (src, dst) in enumerate(kinds):
        copy = pltpu.make_async_copy(src.at[z], dst.at[0, 0, slot(0)], local.at[3 + kind])
        copy.start()
        own.append(copy)
    planes = {}
    for i in range(1, NZ):
        dz = (-Z_ORDER[i]) % NZ
        planes[i] = [
            send(
                src.at[(z + dz) % NZ],
                dst.at[i, 0, slot(0)],
                (zsend, zrecv),
                (i - 1) * 2 + kind,
                dz=dz,
            )
            for kind, (src, dst) in enumerate(kinds)
        ]

    stages = [
        [dict(dc=1)],
        [dict(dx=d) for d in range(1, NX)],
        [dict(dy=d) for d in range(1, NY)],
        [dict(dz=d) for d in range(1, NZ)],
    ]
    load_copies = {}

    def load_send(stage):
        base = sum(len(s) for s in stages[:stage])
        load_copies[stage] = [
            send(lsum.at[stage], lgot.at[base + n], (lsend, lrecv), base + n, **peer)
            for n, peer in enumerate(stages[stage])
        ]

    def load_sum(stage):
        base = sum(len(s) for s in stages[:stage])
        total = lsum[stage]
        arrived(load_copies[stage])
        for n in range(len(stages[stage])):
            total = total + lgot[base + n]
        lsum[stage + 1] = total

    around, onward, across, shares, shared = {}, {}, {}, {}, {}

    def arrive_plane(i):
        if i == 0:
            for copy in own:
                copy.wait()
        else:
            arrived(planes[i])
        around[i] = [
            send(
                buf.at[i, 0, slot(0)],
                buf.at[i, 0, slot((-dy) % NY)],
                (ysend, yrecv),
                i * 6 + n * 2 + kind,
                dy=dy,
            )
            for n, dy in enumerate((1, -1))
            for kind, buf in enumerate((xt, xg))
        ]

    def pass_on(i):
        arrived(around[i])
        onward[i] = [
            send(
                buf.at[i, 0, slot((-dy) % NY)],
                buf.at[i, 0, slot(2)],
                (ysend, yrecv),
                i * 6 + 4 + n,
                dy=dy,
            )
            for n, (dy, buf) in enumerate(((1, xt), (-1, xg)))
        ]

    def cross(i):
        arrived(onward[i])
        across[i] = [
            send(buf.at[i, 0], buf.at[i, 1], (csend, crecv), i * 2 + kind, dc=1)
            for kind, buf in enumerate((xt, xg))
        ]
        shares[i] = [
            send(
                xt.at[i, 0, :, pl.ds(pl.multiple_of(((x + d) % NX) * share, LANE), share)],
                tx.at[(-d) % NX - 1, i, 0],
                (tsend, trecv),
                i * 3 + d - 1,
                dx=d,
            )
            for d in (1, 3, 2)
        ]

    def share_cores(i):
        arrived(shares[i])
        shared[i] = send(tx.at[:, i, 0], tx.at[:, i, 1], (usend, urecv), i, dc=1)

    def forward(g):
        steps = pl.ds(g * GROUP_STEPS, GROUP_STEPS)
        rows = pl.ds(g * GROUP_ROWS, GROUP_ROWS)
        row_in = xt[steps].reshape(GROUP_ROWS, width)
        row_grad = xg[steps].reshape(GROUP_ROWS, width + LANE)
        pre_gate = dot(row_in, wg[...])
        pre_up = dot(row_in, wu[...])
        back_proj = dot_nt(row_grad[:, :width], wd[...])
        gate = row_grad[:, width:].astype(F32)[:, :1]
        sig = 1.0 / (1.0 + jnp.exp(-pre_gate))
        act = pre_gate * sig
        hidden = act * pre_up
        part = jnp.sum(back_proj * hidden, axis=1, keepdims=True)
        scaled = gate * back_proj
        g_gate = scaled * pre_up * sig * (1.0 + pre_gate * (1.0 - sig))
        g_up = scaled * act
        gcat[rows, :units] = g_gate.astype(BF16)
        gcat[rows, units:] = g_up.astype(BF16)
        gt[:units, rows] = jnp.transpose(g_gate).astype(BF16)
        gt[units : 2 * units, rows] = jnp.transpose(g_up).astype(BF16)
        gt[2 * units :, rows] = jnp.transpose(gate * hidden).astype(BF16)
        wide = jnp.broadcast_to(part, (GROUP_ROWS, LANE)).astype(BF16)
        put_dx(g, pl.ds(width, LANE), wide)

    direct, relayed = {}, {}

    def units_out(g):
        rows = pl.ds(g * GROUP_ROWS, GROUP_ROWS)
        both = pl.ds(0, 2 * units)
        direct[g] = [
            send(gt.at[both, rows], gx.at[(-d) % NX - 1, :, rows], (gsend, grecv), g * 4 + n, dx=d)
            for n, d in enumerate((1, 3))
        ]

    def units_on(g):
        rows = pl.ds(g * GROUP_ROWS, GROUP_ROWS)
        arrived(direct[g])
        relayed[g] = [
            send(
                gx.at[(-d) % NX - 1, pl.ds(n * units, units), rows],
                gx.at[1, pl.ds(n * units, units), rows],
                (gsend, grecv),
                g * 4 + 2 + n,
                dx=d,
            )
            for n, d in enumerate((1, 3))
        ]

    def put_dx(g, columns, value):
        value = value.reshape(GROUP_STEPS, NC, NY * CAP, value.shape[1])
        for s in range(GROUP_STEPS):
            dx_keep[g * GROUP_STEPS + s, :, columns] = value[s, 0]
            dx_send[g * GROUP_STEPS + s, :, columns] = value[s, 1]

    dx_tile = 512
    pairs, halves, wholes, returns = {}, {}, {}, []

    def token_part(g):
        rows = pl.ds(g * GROUP_ROWS, GROUP_ROWS)
        for t in range(width // dx_tile):
            columns = pl.ds(t * dx_tile, dx_tile)
            value = dot_nt(gcat[rows, :units], wg[columns, :])
            value = value + dot_nt(gcat[rows, units:], wu[columns, :])
            put_dx(g, columns, value.astype(BF16))
        block = pl.ds(g * GROUP_STEPS, GROUP_STEPS)
        pairs[g] = send(dx_send.at[block], dx_got.at[block], (dsend, drecv), g, dc=1)

    def return_a(g):
        arrived([pairs[g]])
        low, high = g * GROUP_STEPS, g * GROUP_STEPS + 1
        for i in (low, high):
            value = (dx_keep[i].astype(F32) + dx_got[i].astype(F32)).astype(BF16)
            for r in range(NY):
                py[r, i] = value[r * CAP : (r + 1) * CAP]
        sems = (rsend, rrecv)
        halves[g] = [
            send(py.at[2, low], rh.at[0, g], sems, g * 6, dy=1),
            send(py.at[2, high], rh.at[1, g], sems, g * 6 + 1, dy=-1),
        ]
        wholes[g] = [
            send(py.at[1, high], ry.at[0, high], sems, g * 6 + 2, dy=1),
            send(py.at[3, low], ry.at[1, low], sems, g * 6 + 3, dy=-1),
        ]

    def return_b(g):
        low, high = g * GROUP_STEPS, g * GROUP_STEPS + 1
        sems = (rsend, rrecv)
        arrived(halves[g][:1])
        py[1, low] = (py[1, low].astype(F32) + rh[0, g].astype(F32)).astype(BF16)
        wholes[g].append(send(py.at[1, low], ry.at[0, low], sems, g * 6 + 4, dy=1))
        arrived(halves[g][1:])
        py[3, high] = (py[3, high].astype(F32) + rh[1, g].astype(F32)).astype(BF16)
        wholes[g].append(send(py.at[3, high], ry.at[1, high], sems, g * 6 + 5, dy=-1))

    mine = pltpu.make_async_copy(zs.at[0], back.at[z], local.at[5])

    def return_c(g):
        arrived(wholes[g])
        for i in range(g * GROUP_STEPS, (g + 1) * GROUP_STEPS):
            total = py[0, i].astype(F32) + ry[0, i].astype(F32) + ry[1, i].astype(F32)
            zs[i] = total.astype(BF16)
            if i == 0:
                mine.start()
            else:
                returns.append(
                    send(zs.at[i], back.at[z], (bsend, brecv), i - 1, dz=Z_ORDER[i])
                )

    load_send(0)
    last = NZ - 1
    for step in range(NZ + 3):
        if step < NZ:
            arrive_plane(step)
        if 0 <= step - 1 < NZ:
            pass_on(step - 1)
        if step - 1 == last:
            return_a(0)
            return_a(1)
        if 0 <= step - 2 < NZ:
            cross(step - 2)
        if step == 2:
            load_sum(0)
            load_send(1)
        if step == 5:
            load_sum(1)
            load_send(2)
        done = step - 3
        if done >= 0:
            arrived(across[done])
            share_cores(done)
            g = done // GROUP_STEPS
            if done == GROUP_STEPS - 1:
                for copy in weights:
                    copy.wait()
            if done % GROUP_STEPS == GROUP_STEPS - 1:
                if g == GROUPS - 1:
                    return_b(0)
                    return_b(1)
                    return_a(2)
                forward(g)
                units_out(g)
            elif g > 0:
                token_part(g - 1)
                units_on(g - 1)

    cut = units // 2
    first, second = pl.ds(0, cut), pl.ds(cut, cut)
    sems = (xsend, xrecv)

    def down_block(r):
        columns = pl.ds(pl.multiple_of(((x + r) % NX) * share, LANE), share)
        return dot(gt[2 * units :, :], xg[:, :, :, columns].reshape(ROWS, share))

    token_part(GROUPS - 1)
    pb[1] = down_block(2).astype(BF16)
    hop_a = send(pb.at[1, first], half.at[0], sems, 0, dx=1)
    hop_b = send(pb.at[1, second], half.at[1], sems, 1, dx=-1)
    return_b(2)
    return_a(3)
    units_on(GROUPS - 1)
    pb[0] = down_block(1).astype(BF16)
    plus = [send(pb.at[0, second], fin.at[0, second], sems, 2, dx=1)]
    pb[2] = down_block(3).astype(BF16)
    minus = [send(pb.at[2, first], fin.at[1, first], sems, 3, dx=-1)]
    return_c(0)
    return_c(1)
    return_b(3)
    return_c(2)
    load_sum(2)
    load_send(3)
    pb_own[...] = down_block(0)

    arrived([hop_a])
    pb[0, first, :] = (pb[0, first, :].astype(F32) + half[0].astype(F32)).astype(BF16)
    plus.append(send(pb.at[0, first], fin.at[0, first], sems, 4, dx=1))
    arrived([hop_b])
    pb[2, second, :] = (pb[2, second, :].astype(F32) + half[1].astype(F32)).astype(BF16)
    minus.append(send(pb.at[2, second], fin.at[1, second], sems, 5, dx=-1))
    return_c(3)

    for i in range(NZ):
        arrived([shared[i]])
    for g in range(GROUPS):
        arrived(relayed[g])
    columns = pl.ds(pl.multiple_of(x * share, LANE), share)
    for m in range(2):
        there = pl.ds(m * units, units)
        total = dot(gt[there, :], xt[:, :, :, columns].reshape(ROWS, share))
        for n in range(NX - 1):
            total = total + dot(gx[n, there, :], tx[n].reshape(ROWS, share))
        both_out[there, :] = total.astype(BF16)

    mine.wait()
    arrived(returns)
    back_out[...] = back[...]
    load_sum(3)
    load_out[...] = lsum[4]
    arrived(plus)
    arrived(minus)
    down_out[...] = (
        pb_own[...] + fin[0].astype(F32) + fin[1].astype(F32)
    ).astype(BF16)

    for copy in sent:
        copy.wait_send()


def finish_kernel(
    back_ref,
    sel_ref,
    hot_ref,
    both_ref,
    down_ref,
    load_ref,
    bias_ref,
    token_out,
    gate_out,
    dgate_out,
    dup_out,
    ddown_out,
    bias_out,
):
    count, width = token_out.shape
    units = ddown_out.shape[0]
    sel = sel_ref[...]
    spread = jnp.transpose(sel).astype(BF16)
    rows = back_ref[...].reshape(NZ * CAP, width + LANE)
    token_out[...] = dot(spread, rows[:, :width]).astype(BF16)
    weighed = sel * rows[:, width:].astype(F32)
    result = jnp.zeros((TOPK, count), F32)
    for j in range(NZ):
        hot = hot_ref[j * TOPK : (j + 1) * TOPK, :]
        result = result + hot * jnp.sum(
            weighed[j * CAP : (j + 1) * CAP], axis=0, keepdims=True
        )
    gate_out[...] = result
    dgate_out[...] = jnp.transpose(both_ref[:units, :])
    dup_out[...] = jnp.transpose(both_ref[units:, :])
    ddown_out[...] = down_ref[...]
    total = load_ref[0:1, :]
    lean = jnp.sum(total, axis=1, keepdims=True) - float(EXPERTS_ALL) * total
    sign = jnp.where(lean > 0.0, 1.0, jnp.where(lean < 0.0, -1.0, 0.0))
    bias_out[...] = bias_ref[...] + BIAS_STEP * sign


def per_device(tokens, out_grad, route, gate_fixed, w_gate, w_up, w_down, router_bias, loads):
    count, width = tokens.shape
    units = w_gate.shape[2]
    share = width // NX
    wide = width + LANE
    side = NY * CAP
    vmem = pl.BlockSpec(memory_space=pltpu.VMEM)
    hbm = pl.BlockSpec(memory_space=pl.ANY)
    shape = jax.ShapeDtypeStruct

    def buffer(*dims, dtype=BF16):
        return pltpu.VMEM(dims, dtype)

    def pair(n):
        return [pltpu.SemaphoreType.DMA((n,))] * 2

    back, sel, hot, both, down, load = pl.pallas_call(
        layer_kernel,
        out_shape=(
            shape((NZ, CAP, wide), BF16),
            shape((NZ * CAP, count), F32),
            shape((NZ * TOPK, count), F32),
            shape((2 * units, share), BF16),
            shape((units, share), BF16),
            shape((CAP, EXPERTS_ALL), F32),
        ),
        in_specs=[vmem] * 5 + [hbm] * 3,
        out_specs=(vmem,) * 6,
        scratch_shapes=[
            buffer(NZ, CAP, width),
            buffer(NZ, CAP, wide),
            buffer(NZ, NC, side, width),
            buffer(NZ, NC, side, wide),
            buffer(NX - 1, NZ, NC, side, share),
            buffer(width, units),
            buffer(width, units),
            buffer(units, width),
            buffer(ROWS, 2 * units),
            buffer(3 * units, ROWS),
            buffer(NX - 1, 2 * units, ROWS),
            buffer(NZ, side, wide),
            buffer(NZ, side, wide),
            buffer(NZ, side, wide),
            buffer(NY, NZ, CAP, wide),
            buffer(2, GROUPS, CAP, wide),
            buffer(2, NZ, CAP, wide),
            buffer(NZ, CAP, wide),
            buffer(NZ, CAP, wide),
            buffer(NX - 1, units, share),
            buffer(units, share, dtype=F32),
            buffer(2, units // 2, share),
            buffer(2, units, share),
            buffer(5, CAP, EXPERTS_ALL, dtype=F32),
            buffer(14, CAP, EXPERTS_ALL, dtype=F32),
            *pair(14),
            *pair(6 * NZ),
            *pair(2 * NZ),
            *pair(3 * NZ),
            *pair(NZ),
            *pair(4 * GROUPS),
            *pair(GROUPS),
            *pair(6 * GROUPS),
            *pair(7),
            *pair(6),
            *pair(14),
            pltpu.SemaphoreType.DMA((6,)),
        ],
        compiler_params=pltpu.CompilerParams(
            collective_id=0, has_side_effects=True, vmem_limit_bytes=60 * 1024 * 1024
        ),
        name="layer",
    )(
        tokens,
        out_grad,
        jnp.transpose(route),
        jnp.transpose(gate_fixed),
        loads,
        w_gate,
        w_up,
        w_down,
    )
    token_grad, gate_grad, d_gate, d_up, d_down, new_bias = pl.pallas_call(
        finish_kernel,
        out_shape=(
            shape((count, width), BF16),
            shape((TOPK, count), F32),
            shape((share, units), BF16),
            shape((share, units), BF16),
            shape((units, share), BF16),
            shape((1, EXPERTS_ALL), F32),
        ),
        in_specs=[vmem] * 7,
        out_specs=(vmem,) * 6,
        compiler_params=pltpu.CompilerParams(vmem_limit_bytes=60 * 1024 * 1024),
        name="finish",
    )(back, sel, hot, both, down, load, router_bias.reshape(1, EXPERTS_ALL))
    return (
        token_grad,
        jnp.transpose(gate_grad),
        d_gate[None],
        d_up[None],
        d_down[None],
        new_bias.reshape(EXPERTS_ALL),
    )


def solution(mesh):
    in_specs = (
        P(("dp", "expert"), None),
        P(("dp", "expert"), None),
        P(("dp", "expert"), None),
        P(("dp", "expert"), None),
        P("expert", None, None),
        P("expert", None, None),
        P("expert", None, None),
        P(),
        P(("dp", "expert"), None),
    )
    out_specs = (
        P(("dp", "expert"), None),
        P(("dp", "expert"), None),
        P("expert", "dp", None),
        P("expert", "dp", None),
        P("expert", None, "dp"),
        P(),
    )
    return jax.shard_map(
        per_device, mesh=mesh, in_specs=in_specs, out_specs=out_specs, check_vma=False
    )
```
